32 devices in a mesh: group: 2 (over x), head: 16 (over z, y, core).
Axes of the slice: x: 2, y: 2, z: 4, core: 2. Of those that a mesh axis runs over, the one named last changes fastest.
Arguments:
- queries: bfloat16 [4096, 64, 192], P(('group', 'head')), parts along dimension 0, may hold values from -20 to 20
- latent: bfloat16 [4096, 512], P(('group', 'head')), parts along dimension 0, may hold values from -6 to 6
- rope_key: bfloat16 [4096, 64], P(('group', 'head')), parts along dimension 0, may hold values from -8 to 8
- key_up: bfloat16 [512, 64, 128], P(None, 'head'), may hold values from -0.25 to 0.25
- value_up: bfloat16 [512, 64, 128], P(None, 'head'), may hold values from -0.25 to 0.25
- first_key: int32 [4096], P('group'), parts along dimension 0, may hold values from 0 to 2047, as said below
- out_grad: bfloat16 [4096, 64, 128], P(('group', 'head')), parts along dimension 0, may hold values from -6 to 6
Outputs:
- query_grad: bfloat16 [4096, 64, 192], P(('group', 'head')), parts along dimension 0
- latent_grad: bfloat16 [4096, 512], P(('group', 'head')), parts along dimension 0
- rope_key_grad: bfloat16 [4096, 64], P(('group', 'head')), parts along dimension 0
- key_up_grad: float32 [1024, 64, 128], P('group', 'head'), parts along dimension 0
- value_up_grad: float32 [1024, 64, 128], P('group', 'head'), parts along dimension 0
The draws below stay inside these ranges and needn't reach their ends.
There are 2 independent parts, one for each index of `group`. The reference program is written for one: setup_inputs(seed, part) draws one part's arguments, and reference() takes and returns one part's arrays. A program takes and returns all parts, laid end to end along the dimension named above; an argument that names none is the same for every part. Nothing has to cross between parts.
Inputs may be any that keep to these rules, and one draw needn't show every extreme that they name: first_key never decreases as i grows, first_key[i] <= i, and i - first_key[i] < 512.
All inputs are finite; a program needn't handle non-finite values.
Results may differ from the reference program's by a relative error of at most 0.024.
Values may be sent and summed in bfloat16 or wider, within the bound.
No kernel may reach another device: no remote copies, remote signals or barrier semaphores. Data moves between devices by JAX's collectives and lax.ppermute only.
A program may use at most 128 MiB of HBM per device.

```python
import math
import jax
import jax.numpy as jnp
from jax import lax

H = 64
LAT = 512
NOPE = 128
ROPE = 64
VD = 128
QK = 192
SEQ = 2048
QBLOCK = 512
SPAN = 512


def shared_draw(key):
    base = jax.random.fold_in(key, 71)
    keys_split = jax.random.split(base, 2)
    rotary = jnp.clip(jax.random.normal(keys_split[1], (SEQ, ROPE), jnp.float32), -6.0, 6.0)
    query_vals = jnp.clip(jax.random.normal(keys_split[0], (SEQ, H, QK), jnp.float32), -6.0, 6.0)
    return (query_vals, rotary)


def draw_queries(key, part):
    return shared_draw(key)[0].astype(jnp.bfloat16)


def draw_rope_key(key, part):
    return shared_draw(key)[1].astype(jnp.bfloat16)


def draw_first_key(key, part):
    stream = jax.random.fold_in(key, 5)
    cuts = jnp.sort(jax.random.randint(stream, (3,), SPAN, SEQ))
    position = jnp.arange(SEQ, dtype=jnp.int32)
    starts = jnp.max(jnp.where(cuts[None, :] <= position[:, None], cuts[None, :], 0), axis=1)
    return jnp.maximum(starts, position - SPAN + 1).astype(jnp.int32)


def block_levels(own_key, shape, pieces, smallest, high):
    level, own = 1.0, jax.random.fold_in(own_key, 6)
    for axis_at, shards_of in pieces:
        heights = jnp.exp(jax.random.uniform(jax.random.fold_in(own, axis_at), (shards_of,), jnp.float32, smallest / len(pieces), high / len(pieces)))
        level = level * jnp.repeat(heights, shape[axis_at] // shards_of).reshape([-1 if axis == axis_at else 1 for axis in range(len(shape))])
    return level


def gaussian(rng, extent, scale, reach, shards=(), held_as=jnp.bfloat16):
    values = scale * jax.random.normal(rng, extent, jnp.float32)
    if shards:
        values = values * block_levels(rng, extent, shards, -0.22, 0.18)
    return jnp.clip(values, -reach, reach).astype(held_as)


def setup_inputs(seed: int = 0, part: int = 0) -> dict:
    splits = jax.random.split(jax.random.key(seed), 8)
    own_keys = jax.random.split(jax.random.fold_in(splits[7], part), 8)
    return {
        "queries": draw_queries(jax.random.fold_in(jax.random.fold_in(splits[7], part), 71), part),
        "latent": gaussian(own_keys[1], (SEQ, LAT), 1.0, 6.0, ((0, 16),)),
        "rope_key": draw_rope_key(jax.random.fold_in(jax.random.fold_in(splits[7], part), 71), part),
        "key_up": gaussian(splits[3], (LAT, H, NOPE), LAT ** -0.5, 0.25, ((1, 16),)),
        "value_up": gaussian(splits[4], (LAT, H, VD), LAT ** -0.5, 0.25, ((1, 16),)),
        "first_key": draw_first_key(jax.random.fold_in(jax.random.fold_in(splits[7], part), 71), part),
        "out_grad": gaussian(own_keys[6], (SEQ, H, VD), 1.0, 6.0, ((0, 16),)),
    }


def reference(queries, latent, rope_key, key_up, value_up, first_key, out_grad):
    wide = jnp.float32
    low = jnp.bfloat16
    score_scale = 1.0 / math.sqrt(QK)
    latent_wide = latent.astype(wide)
    key_nope = jnp.einsum('tc,chd->thd', latent_wide, key_up.astype(wide)).astype(low)
    values = jnp.einsum('tc,chd->thd', latent_wide, value_up.astype(wide)).astype(low)
    keys_all = jnp.concatenate([key_nope, jnp.broadcast_to(rope_key[:, None, :], (SEQ, H, ROPE))], axis=2)
    window = QBLOCK + SPAN
    block_count = SEQ // QBLOCK

    def backward_block(carry, block_index):
        key_grad, value_grad = carry
        first_row = (block_index * QBLOCK).astype(jnp.int32)
        first_col = jnp.maximum(first_row - SPAN, 0).astype(jnp.int32)
        query_block = lax.dynamic_slice_in_dim(queries, first_row, QBLOCK, 0).astype(wide)
        grad_block = lax.dynamic_slice_in_dim(out_grad, first_row, QBLOCK, 0).astype(wide)
        key_block = lax.dynamic_slice_in_dim(keys_all, first_col, window, 0).astype(wide)
        value_block = lax.dynamic_slice_in_dim(values, first_col, window, 0).astype(wide)
        limits = lax.dynamic_slice_in_dim(first_key, first_row, QBLOCK, 0)
        row_pos = first_row + jnp.arange(QBLOCK, dtype=jnp.int32)
        col_pos = first_col + jnp.arange(window, dtype=jnp.int32)
        visible = (col_pos[None, :] >= limits[:, None]) & (col_pos[None, :] <= row_pos[:, None])
        scores = jnp.einsum('ihd,jhd->hij', query_block, key_block) * score_scale
        scores = jnp.where(visible[None], scores, -jnp.inf)
        peak = lax.optimization_barrier(jnp.max(scores, axis=2, keepdims=True))
        log_total = peak + jnp.log(lax.optimization_barrier(jnp.sum(jnp.exp(scores - peak), axis=2, keepdims=True)))
        probs = jnp.exp(scores - log_total)
        probs_low = probs.astype(low).astype(wide)
        attended = jnp.einsum('hij,jhd->ihd', probs_low, value_block)
        delta = lax.optimization_barrier(jnp.sum(grad_block * attended, axis=2)).T[:, :, None]
        prob_grad = jnp.einsum('ihd,jhd->hij', grad_block, value_block)
        score_grad = (probs * (prob_grad - delta)).astype(low).astype(wide)
        block_qgrad = (score_scale * jnp.einsum('hij,jhd->ihd', score_grad, key_block)).astype(low)
        block_kgrad = score_scale * jnp.einsum('hij,ihd->jhd', score_grad, query_block)
        block_vgrad = jnp.einsum('hij,ihd->jhd', probs_low, grad_block)
        key_grad = lax.dynamic_update_slice_in_dim(key_grad, lax.dynamic_slice_in_dim(key_grad, first_col, window, 0) + block_kgrad, first_col, 0)
        value_grad = lax.dynamic_update_slice_in_dim(value_grad, lax.dynamic_slice_in_dim(value_grad, first_col, window, 0) + block_vgrad, first_col, 0)
        return ((key_grad, value_grad), block_qgrad)
    start = (jnp.zeros((SEQ, H, QK), wide), jnp.zeros((SEQ, H, VD), wide))
    (key_grad, value_grad), query_blocks = lax.scan(backward_block, start, jnp.arange(block_count, dtype=jnp.int32))
    query_grad = query_blocks.reshape(SEQ, H, QK)
    key_low = key_grad.astype(low).astype(wide)
    value_low = value_grad.astype(low).astype(wide)
    key_part = key_low[:, :, :NOPE]
    key_up_grad = jnp.einsum('tc,thd->chd', latent_wide, key_part)
    value_up_grad = jnp.einsum('tc,thd->chd', latent_wide, value_low)
    latent_grad = jnp.einsum('thd,chd->tc', key_part, key_up.astype(wide)) + jnp.einsum('thd,chd->tc', value_low, value_up.astype(wide))
    rope_key_grad = lax.optimization_barrier(jnp.sum(key_low[:, :, NOPE:], axis=1))
    return (query_grad, latent_grad.astype(low), rope_key_grad.astype(low), key_up_grad, value_up_grad)
```

```python
import functools
import math

import jax
import jax.numpy as jnp
from jax import lax
from jax.experimental import pallas as pl
from jax.experimental.pallas import tpu as pltpu
from jax.sharding import PartitionSpec as P

WIDE = jnp.float32
LOW = jnp.bfloat16
PLANE = 4
NT = (((1,), (1,)), ((), ()))
NN = (((1,), (0,)), ((), ()))


def dot(a, b, dims):
    return lax.dot_general(a, b, dims, preferred_element_type=WIDE)


def step_kernel(
    heads, nope, rope, vd, rows,
    pos_ref, x0, x1, x2, x3, w_ref, latr_ref, latt_ref, first_ref, dlat_in,
    y0, y1, y2, y3, dw_ref, dlat_ref,
    q_s, do_s, k_s, v_s, kt_s, dk_s, dv_s, dq_s, bias_s, dkb_s, dvb_s,
):
    width = latt_ref.shape[0]
    qk = nope + rope
    scale = 1.0 / math.sqrt(qk)
    keys = latr_ref.shape[0]
    block = first_ref.shape[2]
    blocks = first_ref.shape[0]
    reach = keys - block * blocks
    window = reach + block
    place = pos_ref[0]
    hn, hv = heads * nope, heads * vd

    for k, x in enumerate((x0, x1, x2, x3)):
        at = pl.ds(pl.multiple_of((place ^ k) * rows, rows), rows)
        for h in range(heads):
            q_s[h, at, :nope] = x[:, h * nope:(h + 1) * nope]
            q_s[h, at, nope:] = x[:, hn + hv + h * rope:hn + hv + (h + 1) * rope]
            do_s[h, at, :] = x[:, hn + h * vd:hn + (h + 1) * vd]

    lat = latr_ref[:, :width]
    key_rope = latr_ref[:, width:]
    key_nope = dot(lat, w_ref[:, :hn], NN).astype(LOW)
    for h in range(heads):
        k_s[h, :, :nope] = key_nope[:, h * nope:(h + 1) * nope]
        k_s[h, :, nope:] = key_rope
    values = dot(lat, w_ref[:, hn:], NN).astype(LOW)
    for h in range(heads):
        v_s[h] = values[:, h * vd:(h + 1) * vd]
    for h in range(heads):
        kt_s[h] = k_s[h].T

    dk_s[...] = jnp.zeros_like(dk_s)
    dv_s[...] = jnp.zeros_like(dv_s)

    for b in range(blocks):
        col = b * block + lax.broadcasted_iota(jnp.int32, (window, block), 0)
        row = b * block + reach + lax.broadcasted_iota(jnp.int32, (window, block), 1)
        seen = (col >= first_ref[b]) & (col <= row)
        bias_s[b] = jnp.where(seen, 0.0, -1e30)

    def attend(i, carry):
        h = i // blocks
        b = i % blocks
        mine = pl.ds(pl.multiple_of(b * block, block), block)
        near = pl.ds(pl.multiple_of(b * block, block), window)
        q = q_s[h, mine, :]
        do = do_s[h, mine, :]
        kw = k_s[h, near, :]
        vw = v_s[h, near, :]
        t = dot(kw, q, NT) * (scale * math.log2(math.e)) + bias_s[b]
        peak = jnp.max(t, axis=0, keepdims=True)
        e = jnp.exp2(t - peak)
        inv = 1.0 / jnp.sum(e, axis=0, keepdims=True)
        probs = e * inv
        dp = dot(vw, do, NT)
        delta = jnp.sum(probs * dp, axis=0, keepdims=True)
        ds = (probs * (dp - delta)).astype(LOW)
        dv_s[h, near, :] += dot(probs.astype(LOW), do, NN)
        dk_s[h, near, :] += dot(ds, q, NN)
        dqt = dot(kt_s[h, :, near], ds, NN) * scale
        dq_s[h, mine, :] = dqt.T.astype(LOW)
        return carry

    lax.fori_loop(0, heads * blocks, attend, 0)

    rope_sum = dlat_in[:, width:]
    for h in range(heads):
        dkh = (dk_s[h] * scale).astype(LOW)
        dkb_s[:, h * nope:(h + 1) * nope] = dkh[:, :nope]
        rope_sum = rope_sum + dkh[:, nope:].astype(WIDE)
        dvb_s[:, h * vd:(h + 1) * vd] = dv_s[h].astype(LOW)
    dlat_ref[:, width:] = rope_sum
    dw_ref[:, :hn] = dot(latt_ref[...], dkb_s[...], NN)
    dw_ref[:, hn:] = dot(latt_ref[...], dvb_s[...], NN)
    dlat_ref[:, :width] = (
        dlat_in[:, :width]
        + dot(dkb_s[...], w_ref[:, :hn], NT)
        + dot(dvb_s[...], w_ref[:, hn:], NT)
    )
    for k, y in enumerate((y0, y1, y2, y3)):
        at = pl.ds(pl.multiple_of((place ^ k) * rows, rows), rows)
        for h in range(heads):
            y[:, h * nope:(h + 1) * nope] = dq_s[h, at, :nope]
            y[:, hn + h * rope:hn + (h + 1) * rope] = dq_s[h, at, nope:]


def attention_step(pos, xs, w, latr, latt, first, dlat, heads, nope, rope, vd):
    rows = xs[0].shape[0]
    keys, both = latr.shape
    width = latt.shape[0]
    blocks, _, block = first.shape
    queries = blocks * block
    window = keys - queries + block
    qk = nope + rope
    vmem = pl.BlockSpec(memory_space=pltpu.VMEM)
    flops = 2 * heads * blocks * block * window * (3 * qk + 2 * vd)
    flops += 6 * keys * width * heads * (nope + vd)
    return pl.pallas_call(
        functools.partial(step_kernel, heads, nope, rope, vd, rows),
        name="attention_step",
        in_specs=[pl.BlockSpec(memory_space=pltpu.SMEM)] + [vmem] * 9,
        out_specs=[vmem] * 6,
        out_shape=[jax.ShapeDtypeStruct((rows, heads * qk), LOW)] * 4
        + [
            jax.ShapeDtypeStruct((width, heads * (nope + vd)), WIDE),
            jax.ShapeDtypeStruct((keys, both), WIDE),
        ],
        scratch_shapes=[
            pltpu.VMEM((heads, queries, qk), LOW),
            pltpu.VMEM((heads, queries, vd), LOW),
            pltpu.VMEM((heads, keys, qk), LOW),
            pltpu.VMEM((heads, keys, vd), LOW),
            pltpu.VMEM((heads, qk, keys), LOW),
            pltpu.VMEM((heads, keys, qk), WIDE),
            pltpu.VMEM((heads, keys, vd), WIDE),
            pltpu.VMEM((heads, queries, qk), LOW),
            pltpu.VMEM((blocks, window, block), WIDE),
            pltpu.VMEM((keys, heads * nope), LOW),
            pltpu.VMEM((keys, heads * vd), LOW),
        ],
        input_output_aliases={9: 5},
        compiler_params=pltpu.CompilerParams(vmem_limit_bytes=50 << 20),
        cost_estimate=pl.CostEstimate(
            flops=flops,
            bytes_accessed=12 << 20,
            transcendentals=heads * blocks * block * window,
        ),
    )(pos, *xs, w, latr, latt, first, dlat)


def shards(queries, latent, rope_key, key_up, value_up, first_key, out_grad):
    rows, all_heads, qk = queries.shape
    devices = lax.axis_size("head")
    width, heads, nope = key_up.shape
    vd = out_grad.shape[2]
    rope = qk - nope
    planes = devices // PLANE
    span = PLANE * rows
    me = lax.axis_index("head")
    plane, place = me // PLANE, me % PLANE
    onward = [(d, (d + PLANE) % devices) for d in range(devices)]
    back = [(d, (d - PLANE) % devices) for d in range(devices)]
    swaps = [[(d, d ^ k) for d in range(devices)] for k in range(PLANE)]

    def swap(value, k):
        return lax.ppermute(value, "head", swaps[k]) if k else value

    def pick(value, index):
        return lax.dynamic_index_in_dim(value, index, 0, keepdims=False)

    weights = [
        jnp.concatenate(
            [key_up.reshape(width, heads * nope), value_up.reshape(width, heads * vd)], axis=1
        )
    ]
    for _ in range(planes - 1):
        weights.append(lax.ppermute(weights[-1], "head", onward))

    own = jnp.concatenate([latent, rope_key], axis=1)
    pair = jnp.stack([lax.ppermute(own, "head", onward), own])
    around = jnp.stack([swap(pair, k) for k in range(PLANE)])
    latr = jnp.concatenate([pick(around, place ^ b) for b in range(PLANE)], axis=1)
    latr = latr.reshape(2 * span, width + rope)
    latt = latr[:, :width].T

    def spread(value):
        return value.reshape(rows, planes, PLANE, -1).transpose(1, 2, 0, 3)

    sends = jnp.concatenate(
        [spread(queries[:, :, :nope]), spread(out_grad), spread(queries[:, :, nope:])], axis=3
    )
    first = lax.dynamic_slice_in_dim(first_key, plane * span, span, 0) - (plane - 1) * span
    first = first.reshape(2, 1, span // 2)
    pos = place.reshape(1).astype(jnp.int32)

    dlat = jnp.zeros((2 * span, width + rope), WIDE)
    grads = jnp.zeros((planes, PLANE, rows, heads * qk), LOW)
    total = None
    mine = None
    order = list(range(1, planes - 1)) + [0, planes - 1]
    for s in order:
        owner = (plane - s) % planes
        chunk = pick(sends, owner)
        xs = [swap(pick(chunk, place ^ k), k) for k in range(PLANE)]
        out = attention_step(
            pos, xs, weights[s], latr, latt, first, dlat, heads, nope, rope, vd
        )
        ys, dw, dlat = out[:4], out[4], out[5]
        for k in range(PLANE):
            grads = lax.dynamic_update_slice(
                grads, swap(ys[k], k)[None, None], (owner, place ^ k, 0, 0)
            )
        if s == 0:
            mine = dw
        else:
            total = dw.astype(LOW) if total is None else (total.astype(WIDE) + dw).astype(LOW)
            total = lax.ppermute(total, "head", onward)

    dw = mine + total.astype(WIDE)
    key_up_grad = dw[:, :heads * nope].reshape(width, heads, nope)
    value_up_grad = dw[:, heads * nope:].reshape(width, heads, vd)

    def gather(value, w):
        return value.transpose(2, 0, 1, 3).reshape(rows, all_heads, w)

    query_out = jnp.concatenate(
        [gather(grads[..., :heads * nope], nope), gather(grads[..., heads * nope:], rope)], axis=2
    )

    part = dlat.astype(LOW).reshape(2, PLANE, rows, width + rope).transpose(1, 0, 2, 3)
    summed = 0.0
    for k in range(PLANE):
        summed = summed + swap(pick(part, place ^ k), k).astype(WIDE)
    moved = lax.ppermute(summed[0].astype(LOW), "head", back).astype(WIDE)
    lat_sum = summed[1] + jnp.where(plane < planes - 1, moved, 0.0)
    lat_sum = lat_sum.astype(LOW)
    return (query_out, lat_sum[:, :width], lat_sum[:, width:], key_up_grad, value_up_grad)


def solution(mesh):
    return jax.shard_map(
        shards,
        mesh=mesh,
        in_specs=(
            P(("group", "head"), None, None),
            P(("group", "head"), None),
            P(("group", "head"), None),
            P(None, "head", None),
            P(None, "head", None),
            P("group"),
            P(("group", "head"), None, None),
        ),
        out_specs=(
            P(("group", "head"), None, None),
            P(("group", "head"), None),
            P(("group", "head"), None),
            P("group", "head", None),
            P("group", "head", None),
        ),
        check_vma=False,
    )
```
